256 devices in a mesh: aux: 32 (over z, x), occ: 8 (over y, core).
Axes of the slice: x: 4, y: 4, z: 8, core: 2. Of those that a mesh axis runs over, the one named last changes fastest.
Arguments:
- half_integrals: float32 [2048, 256, 768], P('aux', 'occ'), may hold values from -2 to 2
- virtual_orbitals: float32 [768, 512], replicated, may hold values from -0.21875 to 0.21875
- occupied_energy: float32 [256], replicated, may hold values from -2 to -0.3
- virtual_energy: float32 [512], replicated, may hold values from 0.3 to 3
- partners: int32 [256, 1], replicated, may hold values from 0 to 255, as said below
Outputs:
- density: float32 [2048, 256, 512], P('aux', 'occ')
The draws below stay inside these ranges and needn't reach their ends.
Inputs may be any that keep to these rules, and one draw needn't show every extreme that they name: `partners`: occupied orbitals form 8 groups of 32 consecutive ones; of the 32 entries of one group, at most 6 lie in any one group, and exactly 6 in some group.
All inputs are finite; a program needn't handle non-finite values.
Results may differ from the reference program's by a relative error of at most 0.00007.
Values sent between devices are 32-bit elements; how exact they have to be, the bound alone decides.
A program may use at most 128 MiB of HBM per device.

```python
import jax
import jax.numpy as jnp
from jax import lax

O = 256
V = 512
AO = 768
NAUX = 2048
NPART = 1
GROUPS = 8
GO = 32


def draw_partners(key, part):
    requests = GO * NPART
    positions = jnp.arange(requests, dtype=jnp.int32)

    def one_group(group):
        group_key = jax.random.fold_in(jax.random.fold_in(key, 7001), group)
        key_target, key_order, key_local = jax.random.split(group_key, 3)
        target = jax.random.randint(key_target, (), 0, GROUPS, dtype=jnp.int32)
        offsets = positions % GROUPS
        first_moved = requests - GROUPS + (target + 1) % GROUPS
        second_moved = requests - GROUPS + (target + 2) % GROUPS
        offsets = jnp.where(positions == first_moved, target, offsets)
        offsets = jnp.where(positions == second_moved, target, offsets)
        order = jax.random.permutation(key_order, requests)
        offsets = offsets[order]
        source_group = (group + offsets) % GROUPS
        local_index = jax.random.randint(key_local, (requests,), 0, GO, dtype=jnp.int32)
        return (source_group * GO + local_index).astype(jnp.int32)
    table = jax.vmap(one_group)(jnp.arange(GROUPS, dtype=jnp.int32))
    return table.reshape(O, NPART)


def shard_levels(rng, shape, shards, smallest, high):
    def one(position, shards_of):
        steps = jax.random.uniform(jax.random.fold_in(jax.random.fold_in(rng, 6), position), (shards_of,), jnp.float32, smallest / len(shards), high / len(shards))
        return jnp.repeat(jnp.exp(steps), shape[position] // shards_of).reshape((-1,) + (1,) * (len(shape) - position - 1))

    gain = one(*shards[0])
    for cut in shards[1:]:
        gain = gain * one(*cut)
    return gain


def centred(stream_key, shape, deviation, bound, shards=(), kind=jnp.bfloat16):
    values = jax.random.normal(stream_key, shape, jnp.float32) * deviation
    if len(shards) > 0:
        values = shard_levels(stream_key, shape, shards, -0.22, 0.18) * values
    return jnp.clip(values, min=-bound, max=bound).astype(kind)


def setup_inputs(seed: int = 0) -> dict:
    key_list = jax.random.split(jax.random.key(seed), 6)
    half_integrals = centred(key_list[0], (NAUX, O, AO), 0.15, 2.0, ((0, 32), (1, 8)), jnp.float32)
    virtual_orbitals = centred(key_list[1], (AO, V), AO ** -0.5, 0.21875, (), jnp.float32)
    occupied_energy = jnp.clip(jax.random.uniform(key_list[2], (O,), jnp.float32, -2.0, -0.3), -2.0, -0.3)
    virtual_energy = jnp.clip(jax.random.uniform(key_list[3], (V,), jnp.float32, 0.3, 3.0), 0.3, 3.0)
    partners = draw_partners(jax.random.fold_in(key_list[5], 71), 0)
    return dict(half_integrals=half_integrals, virtual_orbitals=virtual_orbitals, occupied_energy=occupied_energy, virtual_energy=virtual_energy, partners=partners)


def reference(half_integrals, virtual_orbitals, occupied_energy, virtual_energy, partners):
    highest = lax.Precision.HIGHEST
    virtual_ints = jnp.einsum("qim,mv->qiv", half_integrals, virtual_orbitals, precision=highest)
    orbital_ids = jnp.arange(O, dtype=jnp.int32)
    partner_sets = jnp.concatenate([orbital_ids[:, None], partners.astype(jnp.int32)], axis=1)

    def one_orbital(orbital):
        members = partner_sets[orbital]
        own_rows = lax.dynamic_index_in_dim(virtual_ints, orbital, 1, keepdims=False)
        member_rows = jnp.take(virtual_ints, members, axis=1)
        pair_ints = jnp.einsum("qa,qkb->kab", own_rows, member_rows, precision=highest)
        denominator = (virtual_energy[None, :, None] + virtual_energy[None, None, :]
                       - occupied_energy[orbital] - jnp.take(occupied_energy, members)[:, None, None])
        amplitude = pair_ints / denominator
        return jnp.einsum("kab,qkb->qa", amplitude, member_rows, precision=highest)

    result = lax.map(one_orbital, orbital_ids)
    return jnp.transpose(result, (1, 0, 2))
```

```python
import jax
import jax.numpy as jnp
from jax import lax
from jax.experimental import pallas as pl
from jax.experimental.pallas import tpu as pltpu
from jax.sharding import PartitionSpec as P

CAPACITY = 6


def take_rows_kernel(rows_ref, x_ref, o_ref):
    o_ref[...] = x_ref[...]


def take_rows(x, rows):
    count = rows.shape[0]
    block = (1,) + x.shape[1:]
    return pl.pallas_call(
        take_rows_kernel,
        out_shape=jax.ShapeDtypeStruct((count,) + x.shape[1:], x.dtype),
        grid_spec=pltpu.PrefetchScalarGridSpec(
            num_scalar_prefetch=1,
            grid=(count,),
            in_specs=[pl.BlockSpec(block, lambda i, r: (r[i], 0, 0))],
            out_specs=pl.BlockSpec(block, lambda i, r: (i, 0, 0)),
        ),
        cost_estimate=pl.CostEstimate(flops=0, bytes_accessed=2 * count * x[0].size * 4, transcendentals=0),
    )(rows, x)


def local(half_integrals, virtual_orbitals, occupied_energy, virtual_energy, partners):
    high = lax.Precision.HIGH
    groups = lax.axis_size("occ")
    columns = lax.axis_size("aux")
    me = lax.axis_index("occ")
    column = lax.axis_index("aux")
    slices, size, _ = half_integrals.shape
    width = virtual_orbitals.shape[1]
    table = partners.reshape(groups, size)
    source = table // size
    index = table % size
    ids = jnp.arange(size, dtype=jnp.int32)
    same = source[:, :, None] == source[:, None, :]
    rank = jnp.sum((same & (ids[:, None] > ids[None, :])[None]).astype(jnp.int32), axis=2)
    slots = jnp.arange(CAPACITY, dtype=jnp.int32)
    match = (source == me)[:, None, :] & (rank[:, None, :] == slots[None, :, None])
    chosen = jnp.sum(jnp.where(match, index[:, None, :], 0), axis=2)
    my_source = lax.dynamic_index_in_dim(source, me, 0, keepdims=False)
    my_rank = lax.dynamic_index_in_dim(rank, me, 0, keepdims=False)
    my_place = lax.rem(my_source - me + groups, groups) * CAPACITY + my_rank

    rows = jnp.einsum("qim,mv->iqv", half_integrals, virtual_orbitals, precision=high)
    received = []
    order = lax.rem(me + jnp.arange(groups, dtype=jnp.int32), groups)
    outbound = take_rows(rows, jnp.take_along_axis(chosen, order[:, None], axis=0).reshape(-1))
    outbound = outbound.reshape(groups, CAPACITY, slices, width)
    own = lax.all_to_all(rows, "aux", split_axis=0, concat_axis=0, tiled=True)
    received = [outbound[0]]
    for d in range(1, groups):
        received.append(
            lax.ppermute(outbound[d], "occ", [(g, (g + d) % groups) for g in range(groups)])
        )
    pieces = jnp.stack([received[(groups - d) % groups] for d in range(groups)])
    partner_rows = take_rows(pieces.reshape(groups * CAPACITY, slices, width), my_place)
    member = lax.all_to_all(partner_rows, "aux", split_axis=0, concat_axis=0, tiled=True)

    first = me * size + column
    orbital_ids = jnp.arange(groups * size, dtype=jnp.int32)
    pick = lambda i: jnp.sum(jnp.where(orbital_ids == i, occupied_energy, jnp.float32(0.0)))
    own_partner = jnp.sum(jnp.where(orbital_ids == first, partners[:, 0], 0))
    own_energy = pick(first)
    partner_energy = pick(own_partner)
    virtual_pair = virtual_energy[:, None] + virtual_energy[None, :]
    own = own.reshape(columns * slices, width)
    member = member.reshape(columns * slices, width)
    self_t = jnp.einsum("qb,qa->ba", own, own, precision=high) / (virtual_pair - (own_energy + own_energy))
    self_term = jnp.einsum("qb,ba->qa", own, self_t, precision=high)
    cross_t = jnp.einsum("qb,qa->ba", member, own, precision=high) / (virtual_pair - (own_energy + partner_energy))
    density = self_term + jnp.einsum("qb,ba->qa", member, cross_t, precision=high)
    density = lax.all_to_all(
        density.reshape(columns, slices, width), "aux", split_axis=0, concat_axis=0, tiled=True
    )
    return jnp.transpose(density, (1, 0, 2))


def solution(mesh):
    return jax.shard_map(
        local,
        mesh=mesh,
        in_specs=(P("aux", "occ", None), P(), P(), P(), P()),
        out_specs=P("aux", "occ", None),
        check_vma=False,
    )
```

```python
import functools

import jax
import jax.numpy as jnp
from jax import lax
from jax.experimental import pallas as pl
from jax.experimental.pallas import tpu as pltpu
from jax.sharding import PartitionSpec as P

MESH = pl.DeviceIdType.MESH
CAPACITY = 6
NZ, NX, NY, NC = 8, 4, 4, 2
GROUPS = NY * NC
PIECE = 64
ROWS = PIECE * NX
WIDTH = 512
PANEL = 128
PANELS = WIDTH // PANEL
PANEL_AT = [sum(WIDTH - PANEL * k for k in range(j)) for j in range(PANELS)]
PACKED = sum(WIDTH - PANEL * k for k in range(PANELS))
OWN, PAR, OUT = 0, 1, 2
F32, BF16 = jnp.float32, jnp.bfloat16


def split(x):
    high = x.astype(BF16)
    return high, (x - high.astype(F32)).astype(BF16)


def dot3(ah, al, bh, bl):
    d = functools.partial(jnp.dot, preferred_element_type=F32)
    return d(ah, bh) + (d(ah, bl) + d(al, bh))


def kernel(
    chosen_ref, place_ref, energy_ref, rows_ref, ve_row_ref, ve_col_ref, out_ref,
    mine, outbound, inbound, own, par, raw, ps, rs, pc, rc, dense, leaf,
    th, tl, rh, rl, fh, fl,
    xs, xr, os, orr, zs, zr, ls,
):
    aux = lax.axis_index("aux")
    occ = lax.axis_index("occ")
    z = aux // NX
    x = lax.rem(aux, NX)
    core = lax.rem(occ, NC)
    sign = 1 - 2 * core
    down = lax.rem(z - sign + NZ, NZ) * NX + x
    up = lax.rem(z + sign + NZ, NZ) * NX + x

    def to_aux(d):
        return {"aux": d, "occ": occ}

    def x_peer(dx):
        return z * NX + lax.rem(x + dx, NX)

    load = pltpu.make_async_copy(rows_ref, mine, ls.at[0])
    load.start()

    barrier = pltpu.get_barrier_semaphore()
    for d in (down, up, x_peer(1), x_peer(2), x_peer(3)):
        pl.semaphore_signal(barrier, inc=1, device_id=to_aux(d), device_id_type=MESH)
    for d in range(1, GROUPS):
        pl.semaphore_signal(
            barrier, inc=1, device_id={"aux": aux, "occ": lax.rem(occ + d, GROUPS)}, device_id_type=MESH
        )
    pl.semaphore_wait(barrier, 5 + GROUPS - 1)
    load.wait()

    def owner_z(n):
        half, odd = n // 2, lax.rem(n, 2)
        r = (1 - odd) * (half - 4) + odd * (3 - half)
        return lax.rem(z + sign * r + NZ, NZ)

    my_rows = pl.ds(pl.multiple_of(x * PIECE, PIECE), PIECE)

    def x_copies(kind, n):
        zo = owner_z(n)
        made = []
        for dx in range(NX):
            xd = lax.rem(x + dx, NX)
            if kind == OUT:
                src = dense.at[n, pl.ds(pl.multiple_of(xd * PIECE, PIECE), PIECE)]
                dst = out_ref.at[zo * NX + x]
            else:
                src = mine.at[zo * NX + xd]
                dst = (own, par)[kind].at[n, my_rows]
            if dx == 0:
                made.append(pltpu.make_async_copy(src, dst, xs.at[kind, n, 0]))
            else:
                made.append(
                    pltpu.make_async_remote_copy(
                        src_ref=src, dst_ref=dst, send_sem=xs.at[kind, n, dx], recv_sem=xr.at[kind, n, dx],
                        device_id=to_aux(x_peer(dx)), device_id_type=MESH,
                    )
                )
        return made

    def x_start(kind, n):
        for c in x_copies(kind, n):
            c.start()

    def x_arrived(kind, n):
        c = x_copies(kind, n)
        c[0].wait()
        for dx in range(1, NX):
            c[dx].wait_recv()

    def x_sent(kind, n):
        for c in x_copies(kind, n)[1:]:
            c.wait_send()

    def occ_copy(d):
        return pltpu.make_async_remote_copy(
            src_ref=outbound.at[d - 1], dst_ref=inbound.at[GROUPS - d],
            send_sem=os.at[d], recv_sem=orr.at[d],
            device_id={"aux": aux, "occ": lax.rem(occ + d, GROUPS)}, device_id_type=MESH,
        )

    def z_copy(kind, t):
        rows = (own, par)[kind]
        p, r = ((ps, rs), (pc, rc))[kind]
        src, dst, d = {
            0: (rows.at[0], raw.at[kind, 0], down),
            1: (rows.at[1], raw.at[kind, 1], up),
            2: (p.at[0], r.at[0], down),
            3: (p.at[1], r.at[1], up),
            4: (p.at[2], r.at[2], down),
            5: (p.at[3], r.at[3], up),
            6: (p.at[4], r.at[4], down),
            7: (p.at[5], r.at[2], up),
            8: (p.at[5], r.at[1], down),
            9: (r.at[2], r.at[0], up),
            10: (r.at[1], r.at[6], down),
            11: (r.at[0], r.at[5], up),
            12: (leaf.at[0], dense.at[0], up),
            13: (leaf.at[1], dense.at[1], down),
        }[t]
        return pltpu.make_async_remote_copy(
            src_ref=src, dst_ref=dst, send_sem=zs.at[kind, t], recv_sem=zr.at[kind, t],
            device_id=to_aux(d), device_id_type=MESH,
        )

    def send(kind, t):
        z_copy(kind, t).start()

    def arrived(kind, t):
        z_copy(kind, t).wait_recv()

    def products(kind, a, b, dst, add):
        rh[...], rl[...] = split(a[...])
        th[...], tl[...] = split(b[...].T)
        if kind == OWN:
            for j in range(PANELS):
                at, cols = PANEL * j, slice(PANEL * j, PANEL * (j + 1))
                v = dot3(th[at:, :], tl[at:, :], rh[:, cols], rl[:, cols])
                rows = slice(PANEL_AT[j], PANEL_AT[j] + WIDTH - at)
                dst[rows, :] = dst[rows, :] + v if add else v
        else:

            @pl.loop(0, 2)
            def _(h):
                rows = pl.ds(pl.multiple_of(h * 256, 256), 256)
                v = dot3(th[rows, :], tl[rows, :], rh[...], rl[...])
                dst[rows, :] = dst[rows, :] + v if add else v

    def partial_products(kind, n):
        x_arrived(kind, n)
        if kind == OWN:
            products(OWN, own.at[n], own.at[n], ps.at[n - 2], False)
        else:
            products(PAR, own.at[n], par.at[n], pc.at[n - 2], False)

    def accumulate(kind, p, r):
        dst, src = ((ps, rs), (pc, rc))[kind]
        dst[p] = dst[p] + src[r]

    def to_amplitude(kind):
        if kind == OWN:
            for j in range(PANELS):
                at = PANEL * j
                rows = slice(PANEL_AT[j], PANEL_AT[j] + WIDTH - at)
                pair = ve_col_ref[at:, :] + ve_row_ref[0:1, at : at + PANEL] - energy_ref[0]
                ps[5, rows, :] = (ps[5, rows, :] + rs[3, rows, :] + rs[4, rows, :]) / pair
        else:
            for j in range(PANELS):
                cols = slice(PANEL * j, PANEL * (j + 1))
                pair = ve_col_ref[...] + ve_row_ref[0:1, cols] - energy_ref[1]
                pc[5, :, cols] = (pc[5, :, cols] + rc[3, :, cols] + rc[4, :, cols]) / pair

    def unpack(kind, p):
        own_t, other_t = ((ps, rs), (pc, rc))[kind]
        t = own_t.at[5] if p == 5 else other_t.at[(5, 6, 0, 1, 2)[p]]
        if kind == OWN:
            for j in range(PANELS):
                at = PANEL * j
                cols = slice(at, at + PANEL)
                v = t[PANEL_AT[j] : PANEL_AT[j] + WIDTH - at, :]
                fh[at:, cols], fl[at:, cols] = split(v)
                for i in range(j + 1, PANELS):
                    over = slice(PANEL * i, PANEL * (i + 1))
                    w = v[PANEL * (i - j) : PANEL * (i - j + 1), :].T
                    fh[cols, over], fl[cols, over] = split(w)
        else:
            fh[...], fl[...] = split(t[...])

    def apply(kind, src, dst):
        rh[...], rl[...] = split(src[...])

        @pl.loop(0, 2)
        def _(h):
            cols = pl.ds(pl.multiple_of(h * 256, 256), 256)
            v = dot3(rh[...], rl[...], fh[:, cols], fl[:, cols])
            dst[:, cols] = v if kind == OWN else dst[:, cols] + v

    def density(kind, p):
        unpack(kind, p)
        apply(kind, (own, par)[kind].at[p + 2], dense.at[p + 2])

    def density_leaf(kind, p):
        unpack(kind, p)
        apply(kind, raw.at[kind, p], leaf.at[p])
        if kind == PAR:
            send(kind, 12 + p)
        apply(kind, (own, par)[kind].at[p + 2], dense.at[p + 2])

    @pl.loop(0, NZ)
    def _(n):
        x_start(OWN, n)

    for d in range(1, GROUPS):

        @pl.loop(0, CAPACITY)
        def _(s):
            outbound[d - 1, s] = mine[chosen_ref[d, s]]

        occ_copy(d).start()

    @pl.loop(0, CAPACITY)
    def _(s):
        inbound[0, s] = mine[chosen_ref[0, s]]

    def inward(kind, between):
        for n in range(2):
            x_arrived(kind, n)
            send(kind, n)
        for n in (2, 3):
            partial_products(kind, n)
        between(0)
        a = raw.at[OWN]
        b = raw.at[kind]
        p = (ps, pc)[kind]
        for j in range(2):
            arrived(kind, j)
            products(kind, a.at[j], b.at[j], p.at[j], True)
            send(kind, 2 + j)
        for n in (4, 5):
            partial_products(kind, n)
        between(1)
        for j in range(2):
            arrived(kind, 2 + j)
            accumulate(kind, 2 + j, j)
            send(kind, 4 + j)
        for n in (6, 7):
            partial_products(kind, n)
        between(2)
        arrived(kind, 4)
        accumulate(kind, 4, 2)
        send(kind, 6)
        between(3)
        arrived(kind, 5)
        arrived(kind, 6)
        to_amplitude(kind)
        send(kind, 7)
        send(kind, 8)

    inward(OWN, lambda k: None)

    @pl.loop(0, NZ)
    def _(n):
        x_sent(OWN, n)

    for d in range(1, GROUPS):
        occ_copy(d).wait_recv()

    @pl.loop(0, NZ)
    def _(n):
        zo = owner_z(n)
        for k in range(NX):
            at = place_ref[zo * NX + k]
            mine[zo * NX + k] = inbound[at // CAPACITY, lax.rem(at, CAPACITY)]
        x_start(PAR, n)

    arrived(OWN, 7)
    send(OWN, 9)
    arrived(OWN, 8)
    send(OWN, 10)
    arrived(OWN, 9)
    send(OWN, 11)

    def between(k):
        if k == 0:
            density(OWN, 5)
            density(OWN, 4)
            density(OWN, 3)
        if k == 1:
            arrived(OWN, 10)
            density_leaf(OWN, 1)
            density(OWN, 2)
        if k == 2:
            arrived(OWN, 11)
            density_leaf(OWN, 0)

    inward(PAR, between)

    arrived(PAR, 7)
    send(PAR, 9)
    arrived(PAR, 8)
    send(PAR, 10)
    density(PAR, 5)
    x_start(OUT, 7)
    arrived(PAR, 9)
    send(PAR, 11)
    density(PAR, 4)
    x_start(OUT, 6)
    density(PAR, 3)
    x_start(OUT, 5)
    arrived(PAR, 10)
    density_leaf(PAR, 1)
    x_start(OUT, 3)
    density(PAR, 2)
    x_start(OUT, 4)
    arrived(PAR, 11)
    density_leaf(PAR, 0)
    x_start(OUT, 2)
    for n in range(2):
        arrived(PAR, 12 + n)
        x_start(OUT, n)

    for kind in (OWN, PAR):
        for t in range(14 if kind == PAR else 12):
            z_copy(kind, t).wait_send()
    for d in range(1, GROUPS):
        occ_copy(d).wait_send()

    @pl.loop(0, NZ)
    def _(n):
        x_sent(PAR, n)
        x_arrived(OUT, n)
        x_sent(OUT, n)


def local(half_integrals, virtual_orbitals, occupied_energy, virtual_energy, partners):
    groups = lax.axis_size("occ")
    me = lax.axis_index("occ")
    column = lax.axis_index("aux")
    slices, size, _ = half_integrals.shape
    width = virtual_orbitals.shape[1]
    table = partners.reshape(groups, size)
    source = table // size
    index = table % size
    ids = jnp.arange(size, dtype=jnp.int32)
    same = source[:, :, None] == source[:, None, :]
    rank = jnp.sum((same & (ids[:, None] > ids[None, :])[None]).astype(jnp.int32), axis=2)
    slots = jnp.arange(CAPACITY, dtype=jnp.int32)
    match = (source == me)[:, None, :] & (rank[:, None, :] == slots[None, :, None])
    chosen = jnp.sum(jnp.where(match, index[:, None, :], 0), axis=2)
    turned = lax.rem(me + jnp.arange(groups, dtype=jnp.int32), groups)
    turn = turned[:, None] == jnp.arange(groups, dtype=jnp.int32)[None, :]
    chosen = jnp.sum(jnp.where(turn[:, :, None], chosen[None], 0), axis=1)
    my_source = lax.dynamic_index_in_dim(source, me, 0, keepdims=False)
    my_rank = lax.dynamic_index_in_dim(rank, me, 0, keepdims=False)
    my_place = lax.rem(my_source - me + groups, groups) * CAPACITY + my_rank

    first = me * size + column
    orbital_ids = jnp.arange(groups * size, dtype=jnp.int32)
    pick = lambda i: jnp.sum(jnp.where(orbital_ids == i, occupied_energy, jnp.float32(0.0)))
    own_energy = pick(first)
    partner_energy = pick(jnp.sum(jnp.where(orbital_ids == first, partners[:, 0], 0)))
    energy = jnp.stack([own_energy + own_energy, own_energy + partner_energy])

    rows = jnp.einsum(
        "qim,mv->iqv", half_integrals, virtual_orbitals, precision=lax.Precision.HIGHEST
    )
    vmem = lambda *s: pltpu.VMEM(s, F32)
    dma = pltpu.SemaphoreType.DMA
    smem = pl.BlockSpec(memory_space=pltpu.SMEM)
    out = pl.pallas_call(
        kernel,
        out_shape=jax.ShapeDtypeStruct((size, slices, width), F32),
        in_specs=[smem, smem, smem, pl.BlockSpec(memory_space=pl.ANY)]
        + [pl.BlockSpec(memory_space=pltpu.VMEM)] * 2,
        out_specs=pl.BlockSpec(memory_space=pl.ANY),
        scratch_shapes=[
            vmem(size, slices, width),
            vmem(GROUPS - 1, CAPACITY, slices, width),
            vmem(GROUPS, CAPACITY, slices, width),
            vmem(NZ, ROWS, WIDTH),
            vmem(NZ, ROWS, WIDTH),
            vmem(2, 2, ROWS, WIDTH),
            vmem(6, PACKED, PANEL),
            vmem(7, PACKED, PANEL),
            vmem(6, WIDTH, WIDTH),
            vmem(7, WIDTH, WIDTH),
            vmem(NZ, ROWS, WIDTH),
            vmem(2, ROWS, WIDTH),
            pltpu.VMEM((WIDTH, ROWS), BF16),
            pltpu.VMEM((WIDTH, ROWS), BF16),
            pltpu.VMEM((ROWS, WIDTH), BF16),
            pltpu.VMEM((ROWS, WIDTH), BF16),
            pltpu.VMEM((WIDTH, WIDTH), BF16),
            pltpu.VMEM((WIDTH, WIDTH), BF16),
            dma((3, NZ, NX)),
            dma((3, NZ, NX)),
            dma((GROUPS,)),
            dma((GROUPS,)),
            dma((2, 14)),
            dma((2, 14)),
            dma((1,)),
        ],
        compiler_params=pltpu.CompilerParams(
            collective_id=0, has_side_effects=True, vmem_limit_bytes=62 * 1024 * 1024
        ),
    )(
        chosen,
        my_place,
        energy,
        rows,
        virtual_energy[None, :],
        jnp.broadcast_to(virtual_energy[:, None], (width, PANEL)),
    )
    return jnp.transpose(out, (1, 0, 2))


def solution(mesh):
    return jax.shard_map(
        local,
        mesh=mesh,
        in_specs=(P("aux", "occ", None), P(), P(), P(), P()),
        out_specs=P("aux", "occ", None),
        check_vma=False,
    )
```

```python
import functools

import jax
import jax.numpy as jnp
from jax import lax
from jax.experimental import pallas as pl
from jax.experimental.pallas import tpu as pltpu
from jax.sharding import PartitionSpec as P

MESH = pl.DeviceIdType.MESH
CAPACITY = 6
NZ, NX, NY, NC = 8, 4, 4, 2
GROUPS = NY * NC
PIECE = 64
GO, SUB = 32, 8
ROWS = PIECE * NX
WIDTH = 512
PANEL = 128
PANELS = WIDTH // PANEL
OFF = [(j, i) for j in range(PANELS) for i in range(j + 1, PANELS)]
SPARE = PANEL * (len(OFF) + PANELS // 2)
PACKED = SPARE + 8
CUTS = ((0, PACKED // 16 * 8, PACKED), (0, WIDTH // 2, WIDTH))
OWN, PAR, OUT = 0, 1, 2
PARTS = 2
F32, BF16 = jnp.float32, jnp.bfloat16


def split(x):
    high = x.astype(BF16)
    return high, (x - high.astype(F32)).astype(BF16)


def dot3(ah, al, bh, bl):
    d = functools.partial(jnp.dot, preferred_element_type=F32)
    return d(ah, bh) + (d(ah, bl) + d(al, bh))


def kernel(
    partners_ref, occupied_ref, partner_row_ref, partner_col_ref, half_ref, orbitals_ref, ve_row_ref, out_ref,
    mine, pool, inbound, own, par, raw, ps, rs, pc, rc,
    th, tl, rh, rl, fh, fl, half, wh, wl, ah, al, vc, table_v, place_v, table_s, place_s,
    xs, xr, os, orr, zs, zr, ls,
):
    aux = lax.axis_index("aux")
    occ = lax.axis_index("occ")
    z = aux // NX
    x = lax.rem(aux, NX)
    core = lax.rem(occ, NC)
    sign = 1 - 2 * core
    z_down = lax.rem(z - sign + NZ, NZ) * NX
    z_up = lax.rem(z + sign + NZ, NZ) * NX
    down, up = z_down + x, z_up + x

    def to_aux(d):
        return {"aux": d, "occ": occ}

    def x_turn(dx):
        return lax.rem(x + dx, NX)

    loads = [
        pltpu.make_async_copy(
            half_ref.at[:, pl.ds(SUB * c, SUB), pl.ds(PANEL * m, PANEL)], half.at[c, m], ls.at[c, m]
        )
        for c in range(half.shape[0])
        for m in range(half.shape[1])
    ]
    for c in loads:
        c.start()

    barrier = pltpu.get_barrier_semaphore()
    near = [z_down + x_turn(k) for k in range(NX)] + [z_up + x_turn(k) for k in range(NX)]
    near += [z * NX + x_turn(k) for k in range(1, NX)]
    for d in near:
        pl.semaphore_signal(barrier, inc=1, device_id=to_aux(d), device_id_type=MESH)
    for d in range(1, GROUPS):
        pl.semaphore_signal(
            barrier, inc=1, device_id={"aux": aux, "occ": lax.rem(occ + d, GROUPS)}, device_id_type=MESH
        )

    wh[...], wl[...] = split(orbitals_ref[...])
    total = GROUPS * GO
    row, col = partner_row_ref[...], partner_col_ref[...]
    shift = lambda v: lax.shift_right_logical(v, jnp.full_like(v, 5))
    lane = lax.broadcasted_iota(jnp.int32, (total, total), 1)
    sub = lax.broadcasted_iota(jnp.int32, (total, total), 0)
    ahead = (shift(col) == shift(row)) & (shift(lane) == shift(sub)) & (sub < lane)
    rank = jnp.sum(jnp.where(ahead, 1, 0), axis=0, keepdims=True)
    source = shift(row)
    place = ((source - occ) & (GROUPS - 1)) * CAPACITY + jnp.minimum(rank, CAPACITY - 1)
    place_v[...] = jnp.broadcast_to(place, (8, total))
    asker = shift(lax.broadcasted_iota(jnp.int32, (GROUPS, total), 1))
    turned = (occ + lax.broadcasted_iota(jnp.int32, (GROUPS, total), 0)) & (GROUPS - 1)
    slot = lax.broadcasted_iota(jnp.int32, (GROUPS, PANEL), 1)
    table = jnp.zeros((GROUPS, PANEL), jnp.int32)
    for s in range(CAPACITY):
        pick = jnp.where((source == occ) & (rank == s), row & (GO - 1), 0)
        found = jnp.sum(jnp.where(asker == turned, pick, 0), axis=1, keepdims=True)
        table = jnp.where(slot == s, found, table)
    table_v[...] = table
    to_table = pltpu.make_async_copy(table_v, table_s, ls.at[4, 0])
    to_place = pltpu.make_async_copy(place_v, place_s, ls.at[4, 1])
    to_table.start()
    to_place.start()
    vc[...] = jnp.broadcast_to(ve_row_ref[...], (PANEL, WIDTH)).T
    first = occ * GO + aux
    own_energy = occupied_ref[first]
    self_energy = own_energy + own_energy
    cross_energy = own_energy + occupied_ref[partners_ref[first]]
    pl.semaphore_wait(barrier, len(near) + GROUPS - 1)
    to_table.wait()
    to_place.wait()
    for c in loads:
        c.wait()

    def owner_z(n):
        half_n, odd = n // 2, lax.rem(n, 2)
        r = (1 - odd) * (half_n - 4) + odd * (3 - half_n)
        return lax.rem(z + sign * r + NZ, NZ)

    def block(ref, i, count=1):
        return ref.at[i] if count == 1 else ref.at[pl.ds(i, count)]

    def rows_of(ref, i):
        return ref.at[pl.ds(pl.multiple_of(i * PIECE, PIECE), PIECE)]

    def dense(n):
        return block(pool, (n - 2) * NX, NX)

    def leaf(j):
        return block(pool, (6 + j) * NX, NX)

    def remote(kind, n, dx, src, dst, d):
        return pltpu.make_async_remote_copy(
            src_ref=src, dst_ref=dst, send_sem=xs.at[kind, n, dx], recv_sem=xr.at[kind, n, dx],
            device_id=to_aux(d), device_id_type=MESH,
        )

    def end_copies(kind, n):
        made = []
        for dx in range(NX):
            xd = x_turn(dx)
            if kind == OUT:
                src = block(leaf(n), xd)
                dst = out_ref.at[owner_z(n + 2) * NX + x]
                d = (z_up, z_down)[n] + xd
            else:
                src = block(mine, owner_z(n) * NX + xd)
                dst = rows_of(raw.at[kind, n], x)
                d = (z_down, z_up)[n] + xd
            made.append(remote(kind, n, dx, src, dst, d))
        return made

    def x_copies(kind, n):
        zo = owner_z(n)
        made = []
        for dx in range(NX):
            xd = x_turn(dx)
            if kind == OUT:
                src = block(pool, (n - 2) * NX + xd)
                dst = out_ref.at[zo * NX + x]
            else:
                src = block(mine, zo * NX + xd)
                dst = rows_of((own, par)[kind].at[n - 2], x)
            if dx == 0:
                made.append(pltpu.make_async_copy(src, dst, xs.at[kind, n, 0]))
            else:
                made.append(remote(kind, n, dx, src, dst, z * NX + xd))
        return made

    def start(copies):
        for c in copies:
            c.start()

    def x_arrived(kind, n):
        c = x_copies(kind, n)
        c[0].wait()
        for dx in range(1, NX):
            c[dx].wait_recv()

    def x_sent(kind, n):
        for c in x_copies(kind, n)[1:]:
            c.wait_send()

    def end_arrived(kind, n):
        for c in end_copies(kind, n):
            c.wait_recv()

    def end_sent(kind, n):
        for c in end_copies(kind, n):
            c.wait_send()

    def occ_copy(d):
        return pltpu.make_async_remote_copy(
            src_ref=block(pool, (d - 1) * CAPACITY, CAPACITY),
            dst_ref=block(inbound, (GROUPS - d) * CAPACITY, CAPACITY),
            send_sem=os.at[d], recv_sem=orr.at[d],
            device_id={"aux": aux, "occ": lax.rem(occ + d, GROUPS)}, device_id_type=MESH,
        )

    def part(kind, h):
        return pl.ds(CUTS[kind][h], CUTS[kind][h + 1] - CUTS[kind][h])

    def z_copy(kind, t, h):
        p, r = ((ps, rs), (pc, rc))[kind]
        src, dst, d = {
            2: (p.at[0], r.at[0], down),
            3: (p.at[1], r.at[1], up),
            4: (p.at[2], r.at[2], down),
            5: (p.at[3], r.at[3], up),
            6: (p.at[4], r.at[4], down),
            7: (p.at[5], r.at[2], up),
            8: (p.at[5], r.at[1], down),
            9: (r.at[2], r.at[0], up),
            10: (r.at[1], r.at[6], down),
            11: (r.at[0], r.at[5], up),
        }[t]
        rows = part(kind, h)
        return pltpu.make_async_remote_copy(
            src_ref=src.at[rows], dst_ref=dst.at[rows], send_sem=zs.at[kind, t, h], recv_sem=zr.at[kind, t, h],
            device_id=to_aux(d), device_id_type=MESH,
        )

    def send(kind, t, h):
        z_copy(kind, t, h).start()

    def arrived(kind, t, h):
        z_copy(kind, t, h).wait_recv()

    def pass_on(kind, t, then):
        for h in range(PARTS):
            arrived(kind, t, h)
            send(kind, then, h)

    def first_product(n):
        zo = owner_z(n)
        for m in range(half.shape[1]):
            at = half.at[zo // 2, m].reshape(PIECE * SUB, PANEL)
            cols = slice(PANEL * m, PANEL * (m + 1))
            for k in range(NX):
                rows = slice(PIECE * k, PIECE * (k + 1))
                v = at[pl.ds(lax.rem(zo, 2) * NX + k, PIECE, stride=SUB), :]
                ah[rows, cols], al[rows, cols] = split(v)

        @pl.loop(0, 2)
        def _(h):
            cols = pl.ds(pl.multiple_of(h * 256, 256), 256)
            v = dot3(ah[...], al[...], wh[:, cols], wl[:, cols])
            for k in range(NX):
                mine[zo * NX + k, :, cols] = v[PIECE * k : PIECE * (k + 1), :]

    tile_row = lax.broadcasted_iota(jnp.int32, (PANEL, PANEL), 0)
    tile_col = lax.broadcasted_iota(jnp.int32, (PANEL, PANEL), 1)
    low, diagonal = tile_row >= tile_col, tile_row == tile_col
    spare = lax.broadcasted_iota(jnp.int32, (8, PANEL), 0)

    def pair_block(i, j):
        return vc[PANEL * i : PANEL * (i + 1), :] + ve_row_ref[0:1, PANEL * j : PANEL * (j + 1)] - self_energy

    def products(kind, a, b, dst, add):
        rh[...], rl[...] = split(a[...])
        th[...], tl[...] = split(b[...].T)
        if kind == OWN:

            def put(at, v):
                rows = slice(at, at + v.shape[0])
                dst[rows, :] = dst[rows, :] + v if add else v

            extra = jnp.zeros((8, PANEL), F32)
            first = None
            for j in range(PANELS):
                at, cols = PANEL * j, slice(PANEL * j, PANEL * (j + 1))
                v = dot3(th[at:, :], tl[at:, :], rh[:, cols], rl[:, cols])
                if j + 1 < PANELS:
                    put(PANEL * OFF.index((j, j + 1)), v[PANEL:, :])
                if j % 2 == 0:
                    first = v[:PANEL, :]
                else:
                    second = v[:PANEL, :]
                    put(PANEL * (len(OFF) + j // 2), jnp.where(low, first, second))
                    d = jnp.sum(jnp.where(diagonal, second, 0.0), axis=0, keepdims=True)
                    extra = jnp.where(spare == j // 2, d, extra)
            put(SPARE, extra)
        else:

            @pl.loop(0, 2)
            def _(h):
                rows = pl.ds(pl.multiple_of(h * 256, 256), 256)
                v = dot3(th[rows, :], tl[rows, :], rh[...], rl[...])
                dst[rows, :] = dst[rows, :] + v if add else v

    def partial_products(kind, n):
        x_arrived(kind, n)
        if kind == OWN:
            products(OWN, own.at[n - 2], own.at[n - 2], ps.at[n - 2], False)
        else:
            products(PAR, own.at[n - 2], par.at[n - 2], pc.at[n - 2], False)

    def accumulate(kind, p, r, h):
        dst, src = ((ps, rs), (pc, rc))[kind]
        rows = part(kind, h)
        dst[p, rows, :] = dst[p, rows, :] + src[r, rows, :]

    def to_amplitude(kind, h):
        if kind == OWN:

            def divide(at, pair):
                rows = slice(at, at + pair.shape[0])
                ps[5, rows, :] = (ps[5, rows, :] + rs[3, rows, :] + rs[4, rows, :]) / pair

            for b, (j, i) in enumerate(OFF):
                if CUTS[OWN][h] <= PANEL * b < CUTS[OWN][h + 1]:
                    divide(PANEL * b, pair_block(i, j))
            if h == PARTS - 1:
                extra = jnp.ones((8, PANEL), F32)
                for k in range(PANELS // 2):
                    i, j = 2 * k, 2 * k + 1
                    divide(PANEL * (len(OFF) + k), jnp.where(low, pair_block(i, i), pair_block(j, j)))
                    ve = ve_row_ref[0:1, PANEL * j : PANEL * (j + 1)]
                    extra = jnp.where(spare == k, ve + ve - self_energy, extra)
                divide(SPARE, extra)
        else:
            rows = part(PAR, h)
            for j in range(PANELS):
                cols = slice(PANEL * j, PANEL * (j + 1))
                pair = vc[rows, :] + ve_row_ref[0:1, cols] - cross_energy
                pc[5, rows, cols] = (pc[5, rows, cols] + rc[3, rows, cols] + rc[4, rows, cols]) / pair

    def unpack(kind, p):
        own_t, other_t = ((ps, rs), (pc, rc))[kind]
        t = own_t.at[5] if p == 5 else other_t.at[(5, 6, 0, 1, 2)[p]]
        if kind == OWN:

            def put(i, j, v):
                at = slice(PANEL * i, PANEL * (i + 1)), slice(PANEL * j, PANEL * (j + 1))
                fh[at], fl[at] = split(v)

            for b, (j, i) in enumerate(OFF):
                v = t[PANEL * b : PANEL * (b + 1), :]
                put(i, j, v)
                put(j, i, v.T)
            for k in range(PANELS // 2):
                at = PANEL * (len(OFF) + k)
                v = t[at : at + PANEL, :]
                w = v.T
                put(2 * k, 2 * k, jnp.where(low, v, w))
                d = t[SPARE + k : SPARE + k + 1, :]
                put(2 * k + 1, 2 * k + 1, jnp.where(diagonal, d, jnp.where(low, w, v)))
        else:
            fh[...], fl[...] = split(t[...])

    def apply(kind, src, dst):
        rh[...], rl[...] = split(src[...])

        @pl.loop(0, 2)
        def _(h):
            cols = pl.ds(pl.multiple_of(h * 256, 256), 256)
            v = dot3(rh[...], rl[...], fh[:, cols], fl[:, cols])
            for k in range(NX):
                w = v[PIECE * k : PIECE * (k + 1), :]
                dst[k, :, cols] = w if kind == OWN else dst[k, :, cols] + w

    def density(kind, p):
        unpack(kind, p)
        apply(kind, (own, par)[kind].at[p], dense(p + 2))

    def density_leaf(kind, p):
        unpack(kind, p)
        apply(kind, raw.at[kind, p], leaf(p))
        if kind == PAR:
            start(end_copies(OUT, p))
        apply(kind, (own, par)[kind].at[p], dense(p + 2))

    def begin_occ():
        for d in range(1, GROUPS):

            @pl.loop(0, CAPACITY)
            def _(s):
                pool[(d - 1) * CAPACITY + s] = mine[table_s[d, s]]

            occ_copy(d).start()

        @pl.loop(0, CAPACITY)
        def _(s):
            inbound[s] = mine[table_s[0, s]]

    def inward(kind, between):
        p = (ps, pc)[kind]
        for j in range(2):
            partial_products(kind, 2 + j)
            end_arrived(kind, j)
            products(kind, raw.at[OWN, j], raw.at[kind, j], p.at[j], True)
            for h in range(PARTS):
                send(kind, 2 + j, h)
            between(j)
        for n in (4, 5):
            partial_products(kind, n)
        between(2)
        for j in range(2):
            for h in range(PARTS):
                arrived(kind, 2 + j, h)
                accumulate(kind, 2 + j, j, h)
                send(kind, 4 + j, h)
        for n in (6, 7):
            partial_products(kind, n)
        between(3)
        for h in range(PARTS):
            arrived(kind, 4, h)
            accumulate(kind, 4, 2, h)
            send(kind, 6, h)
        between(4)
        for h in range(PARTS):
            arrived(kind, 5, h)
            arrived(kind, 6, h)
            to_amplitude(kind, h)
            send(kind, 7, h)
            send(kind, 8, h)

    @pl.loop(0, 2)
    def _(j):
        @pl.loop(0, 2)
        def _(i):
            first_product(2 * i + j)

        for n in range(2):

            @pl.when(j == n)
            def _():
                start(end_copies(OWN, n))

        start(x_copies(OWN, 2 + j))

    @pl.loop(4, NZ)
    def _(n):
        first_product(n)

    begin_occ()

    def rest(k):
        if k < 2:
            start(x_copies(OWN, 4 + k))
            start(x_copies(OWN, 6 + k))

    inward(OWN, rest)

    pass_on(OWN, 7, 9)
    pass_on(OWN, 8, 10)

    for n in range(2):
        end_sent(OWN, n)

    @pl.loop(2, NZ)
    def _(n):
        x_sent(OWN, n)

    for d in range(1, GROUPS):
        occ_copy(d).wait_recv()
        occ_copy(d).wait_send()

    def take_partners(n):
        zo = owner_z(n)
        for k in range(NX):
            mine[zo * NX + k] = inbound[place_s[0, occ * GO + zo * NX + k]]

    for n in range(2):
        take_partners(n)
        start(end_copies(PAR, n))
        take_partners(n + 2)
        start(x_copies(PAR, n + 2))

    pass_on(OWN, 9, 11)

    @pl.loop(4, NZ)
    def _(n):
        take_partners(n)

    def between(k):
        if k < 2:
            start(x_copies(PAR, 4 + k))
            start(x_copies(PAR, 6 + k))
        if k == 0:
            density(OWN, 5)
        if k == 2:
            density(OWN, 4)
            density(OWN, 3)
        if k == 3:
            for h in range(PARTS):
                arrived(OWN, 10, h)
            density_leaf(OWN, 1)
            density(OWN, 2)
        if k == 4:
            for h in range(PARTS):
                arrived(OWN, 11, h)
            density_leaf(OWN, 0)

    inward(PAR, between)

    pass_on(PAR, 7, 9)
    pass_on(PAR, 8, 10)
    density(PAR, 5)
    start(x_copies(OUT, 7))
    pass_on(PAR, 9, 11)
    density(PAR, 4)
    start(x_copies(OUT, 6))
    density(PAR, 3)
    start(x_copies(OUT, 5))
    for h in range(PARTS):
        arrived(PAR, 10, h)
    density_leaf(PAR, 1)
    start(x_copies(OUT, 3))
    density(PAR, 2)
    start(x_copies(OUT, 4))
    for h in range(PARTS):
        arrived(PAR, 11, h)
    density_leaf(PAR, 0)
    start(x_copies(OUT, 2))

    for kind in (OWN, PAR):
        for t in range(2, 12):
            for h in range(PARTS):
                z_copy(kind, t, h).wait_send()

    for n in range(2):
        end_sent(PAR, n)
        end_arrived(OUT, n)
        end_sent(OUT, n)

    @pl.loop(2, NZ)
    def _(n):
        x_sent(PAR, n)
        x_arrived(OUT, n)
        x_sent(OUT, n)


def local(half_integrals, virtual_orbitals, occupied_energy, virtual_energy, partners):
    slices, size, atoms = half_integrals.shape
    width = virtual_orbitals.shape[1]
    total = partners.shape[0]
    vmem = lambda *s: pltpu.VMEM(s, F32)
    half_vmem = lambda *s: pltpu.VMEM(s, BF16)
    dma = pltpu.SemaphoreType.DMA
    smem = pl.BlockSpec(memory_space=pltpu.SMEM)
    whole = pl.BlockSpec(memory_space=pltpu.VMEM)
    hbm = pl.BlockSpec(memory_space=pl.ANY)
    flat = partners.reshape(total)
    out = pl.pallas_call(
        kernel,
        out_shape=jax.ShapeDtypeStruct((size, slices, width), F32),
        in_specs=[smem, smem, whole, whole, hbm, whole, whole],
        out_specs=hbm,
        scratch_shapes=[
            vmem(size, slices, width),
            vmem((GROUPS - 1) * CAPACITY, slices, width),
            vmem(GROUPS * CAPACITY, slices, width),
            vmem(NZ - 2, ROWS, WIDTH),
            vmem(NZ - 2, ROWS, WIDTH),
            vmem(2, 2, ROWS, WIDTH),
            vmem(6, PACKED, PANEL),
            vmem(7, PACKED, PANEL),
            vmem(6, WIDTH, WIDTH),
            vmem(7, WIDTH, WIDTH),
            half_vmem(WIDTH, ROWS),
            half_vmem(WIDTH, ROWS),
            half_vmem(ROWS, WIDTH),
            half_vmem(ROWS, WIDTH),
            half_vmem(WIDTH, WIDTH),
            half_vmem(WIDTH, WIDTH),
            vmem(size // SUB, atoms // PANEL, slices, SUB, PANEL),
            half_vmem(atoms, width),
            half_vmem(atoms, width),
            half_vmem(ROWS, atoms),
            half_vmem(ROWS, atoms),
            vmem(WIDTH, PANEL),
            pltpu.VMEM((GROUPS, PANEL), jnp.int32),
            pltpu.VMEM((8, total), jnp.int32),
            pltpu.SMEM((GROUPS, PANEL), jnp.int32),
            pltpu.SMEM((8, total), jnp.int32),
            dma((3, NZ, NX)),
            dma((3, NZ, NX)),
            dma((GROUPS,)),
            dma((GROUPS,)),
            dma((2, 12, PARTS)),
            dma((2, 12, PARTS)),
            dma((size // SUB + 1, atoms // PANEL)),
        ],
        compiler_params=pltpu.CompilerParams(
            collective_id=0, has_side_effects=True, vmem_limit_bytes=62 * 1024 * 1024
        ),
    )(
        flat,
        occupied_energy,
        flat[None, :],
        partners,
        half_integrals,
        virtual_orbitals,
        virtual_energy[None, :],
    )
    return jnp.transpose(out, (1, 0, 2))


def solution(mesh):
    return jax.shard_map(
        local,
        mesh=mesh,
        in_specs=(P("aux", "occ", None), P(), P(), P(), P()),
        out_specs=P("aux", "occ", None),
        check_vma=False,
    )
```

```python
import functools

import jax
import jax.numpy as jnp
from jax import lax
from jax.experimental import pallas as pl
from jax.experimental.pallas import tpu as pltpu
from jax.sharding import PartitionSpec as P

MESH = pl.DeviceIdType.MESH
CAPACITY = 6
NZ, NX, NY, NC = 8, 4, 4, 2
GROUPS = NY * NC
PIECE = 64
GO, SUB = 32, 8
ROWS = PIECE * NX
WIDTH = 512
PANEL = 128
PANELS = WIDTH // PANEL
OFF = [(j, i) for j in range(PANELS) for i in range(j + 1, PANELS)]
SPARE = PANEL * (len(OFF) + PANELS // 2)
PACKED = SPARE + 8
CUTS = ((0, PACKED // 16 * 8, PACKED), (0, WIDTH // 2, WIDTH))
OWN, PAR, OUT = 0, 1, 2
PARTS = 2
F32, BF16 = jnp.float32, jnp.bfloat16


def split(x):
    high = x.astype(BF16)
    return high, (x - high.astype(F32)).astype(BF16)


def dot3(ah, al, bh, bl):
    d = functools.partial(jnp.dot, preferred_element_type=F32)
    return d(ah, bh) + (d(ah, bl) + d(al, bh))


def kernel(
    partners_ref, occupied_ref, partner_row_ref, partner_col_ref, half_ref, orbitals_ref, ve_row_ref, out_ref,
    mine, pool, inbound, own, par, raw, ps, rs, pc, rc,
    th, tl, rh, rl, fh, fl, half, wh, wl, ah, al, vc, table_v, place_v, table_s, place_s,
    xs, xr, os, orr, zs, zr, ls,
):
    aux = lax.axis_index("aux")
    occ = lax.axis_index("occ")
    z = aux // NX
    x = lax.rem(aux, NX)
    core = lax.rem(occ, NC)
    sign = 1 - 2 * core
    z_down = lax.rem(z - sign + NZ, NZ) * NX
    z_up = lax.rem(z + sign + NZ, NZ) * NX
    down, up = z_down + x, z_up + x

    def to_aux(d):
        return {"aux": d, "occ": occ}

    def x_turn(dx):
        return lax.rem(x + dx, NX)

    loads = [
        pltpu.make_async_copy(
            half_ref.at[:, pl.ds(SUB * c, SUB), pl.ds(PANEL * m, PANEL)], half.at[c, m], ls.at[c, m]
        )
        for c in range(half.shape[0])
        for m in range(half.shape[1])
    ]
    for c in loads:
        c.start()

    barrier = pltpu.get_barrier_semaphore()
    near = [z_down + x_turn(k) for k in range(NX)] + [z_up + x_turn(k) for k in range(NX)]
    near += [z * NX + x_turn(k) for k in range(1, NX)]
    for d in near:
        pl.semaphore_signal(barrier, inc=1, device_id=to_aux(d), device_id_type=MESH)
    for d in range(1, GROUPS):
        pl.semaphore_signal(
            barrier, inc=1, device_id={"aux": aux, "occ": lax.rem(occ + d, GROUPS)}, device_id_type=MESH
        )

    wh[...], wl[...] = split(orbitals_ref[...])
    total = GROUPS * GO
    row, col = partner_row_ref[...], partner_col_ref[...]
    shift = lambda v: lax.shift_right_logical(v, jnp.full_like(v, 5))
    lane = lax.broadcasted_iota(jnp.int32, (total, total), 1)
    sub = lax.broadcasted_iota(jnp.int32, (total, total), 0)


    def use_order(request):
        side = 1 - 2 * (shift(request) & (NC - 1))
        away = (lax.shift_right_logical(request, jnp.full_like(request, 2)) & (NZ - 1)) - z
        r = ((side * away + 4) & (NZ - 1)) - 4
        return jnp.where(r < 0, 2 * (r + 4), 7 - 2 * r) * NX + (request & (NX - 1))

    ahead = (shift(col) == shift(row)) & (shift(lane) == shift(sub)) & (use_order(sub) < use_order(lane))
    rank = jnp.sum(jnp.where(ahead, 1, 0), axis=0, keepdims=True)
    source = shift(row)
    place = ((source - occ) & (GROUPS - 1)) * CAPACITY + jnp.minimum(rank, CAPACITY - 1)
    place_v[...] = jnp.broadcast_to(place, (8, total))
    asker = shift(lax.broadcasted_iota(jnp.int32, (GROUPS, total), 1))
    turned = (occ + lax.broadcasted_iota(jnp.int32, (GROUPS, total), 0)) & (GROUPS - 1)
    slot = lax.broadcasted_iota(jnp.int32, (GROUPS, PANEL), 1)
    table = jnp.zeros((GROUPS, PANEL), jnp.int32)
    for s in range(CAPACITY):
        pick = jnp.where((source == occ) & (rank == s), row & (GO - 1), 0)
        found = jnp.sum(jnp.where(asker == turned, pick, 0), axis=1, keepdims=True)
        table = jnp.where(slot == s, found, table)
    table_v[...] = table
    to_table = pltpu.make_async_copy(table_v, table_s, ls.at[4, 0])
    to_place = pltpu.make_async_copy(place_v, place_s, ls.at[4, 1])
    to_table.start()
    to_place.start()
    vc[...] = jnp.broadcast_to(ve_row_ref[...], (PANEL, WIDTH)).T
    first = occ * GO + aux
    own_energy = occupied_ref[first]
    self_energy = own_energy + own_energy
    cross_energy = own_energy + occupied_ref[partners_ref[first]]
    for c in loads:
        c.wait()

    def owner_z(n):
        half_n, odd = n // 2, lax.rem(n, 2)
        r = (1 - odd) * (half_n - 4) + odd * (3 - half_n)
        return lax.rem(z + sign * r + NZ, NZ)

    def block(ref, i, count=1):
        return ref.at[i] if count == 1 else ref.at[pl.ds(i, count)]

    def rows_of(ref, i):
        return ref.at[pl.ds(pl.multiple_of(i * PIECE, PIECE), PIECE)]

    def dense(n):
        return block(pool, (n - 2) * NX, NX)

    def leaf(j):
        return block(pool, (6 + j) * NX, NX)

    def remote(kind, n, dx, src, dst, d):
        return pltpu.make_async_remote_copy(
            src_ref=src, dst_ref=dst, send_sem=xs.at[kind, n, dx], recv_sem=xr.at[kind, n, dx],
            device_id=to_aux(d), device_id_type=MESH,
        )

    def end_copies(kind, n):
        made = []
        for dx in range(NX):
            xd = x_turn(dx)
            if kind == OUT:
                src = block(leaf(n), xd)
                dst = out_ref.at[owner_z(n + 2) * NX + x]
                d = (z_up, z_down)[n] + xd
            else:
                src = block(mine, owner_z(n) * NX + xd)
                dst = rows_of(raw.at[kind, n], x)
                d = (z_down, z_up)[n] + xd
            made.append(remote(kind, n, dx, src, dst, d))
        return made

    def x_copies(kind, n):
        zo = owner_z(n)
        made = []
        for dx in range(NX):
            xd = x_turn(dx)
            if kind == OUT:
                src = block(pool, (n - 2) * NX + xd)
                dst = out_ref.at[zo * NX + x]
            else:
                src = block(mine, zo * NX + xd)
                dst = rows_of((own, par)[kind].at[n - 2], x)
            if dx == 0:
                made.append(pltpu.make_async_copy(src, dst, xs.at[kind, n, 0]))
            else:
                made.append(remote(kind, n, dx, src, dst, z * NX + xd))
        return made

    def start(copies):
        for c in copies:
            c.start()

    def x_arrived(kind, n):
        c = x_copies(kind, n)
        c[0].wait()
        for dx in range(1, NX):
            c[dx].wait_recv()

    def x_sent(kind, n):
        for c in x_copies(kind, n)[1:]:
            c.wait_send()

    def end_arrived(kind, n):
        for c in end_copies(kind, n):
            c.wait_recv()

    def end_sent(kind, n):
        for c in end_copies(kind, n):
            c.wait_send()

    def occ_copy(d, h):
        first_slot, count = ((0, NX), (NX, CAPACITY - NX))[h]
        return pltpu.make_async_remote_copy(
            src_ref=block(pool, (d - 1) * CAPACITY + first_slot, count),
            dst_ref=block(inbound, (GROUPS - d) * CAPACITY + first_slot, count),
            send_sem=os.at[d, h], recv_sem=orr.at[d, h],
            device_id={"aux": aux, "occ": lax.rem(occ + d, GROUPS)}, device_id_type=MESH,
        )

    def part(kind, h):
        return pl.ds(CUTS[kind][h], CUTS[kind][h + 1] - CUTS[kind][h])

    def z_copy(kind, t, h):
        p, r = ((ps, rs), (pc, rc))[kind]
        src, dst, d = {
            2: (p.at[0], r.at[0], down),
            3: (p.at[1], r.at[1], up),
            4: (p.at[2], r.at[2], down),
            5: (p.at[3], r.at[3], up),
            6: (p.at[4], r.at[4], down),
            7: (p.at[5], r.at[2], up),
            8: (p.at[5], r.at[1], down),
            9: (r.at[2], r.at[0], up),
            10: (r.at[1], r.at[6], down),
            11: (r.at[0], r.at[5], up),
        }[t]
        rows = part(kind, h)
        return pltpu.make_async_remote_copy(
            src_ref=src.at[rows], dst_ref=dst.at[rows], send_sem=zs.at[kind, t, h], recv_sem=zr.at[kind, t, h],
            device_id=to_aux(d), device_id_type=MESH,
        )

    def send(kind, t, h):
        z_copy(kind, t, h).start()

    def arrived(kind, t, h):
        z_copy(kind, t, h).wait_recv()

    def pass_on(kind, *pairs):
        for h in range(PARTS):
            for t, then in pairs:
                arrived(kind, t, h)
                send(kind, then, h)

    def first_product(n):
        zo = owner_z(n)
        for m in range(half.shape[1]):
            at = half.at[zo // 2, m].reshape(PIECE * SUB, PANEL)
            cols = slice(PANEL * m, PANEL * (m + 1))
            for k in range(NX):
                rows = slice(PIECE * k, PIECE * (k + 1))
                v = at[pl.ds(lax.rem(zo, 2) * NX + k, PIECE, stride=SUB), :]
                ah[rows, cols], al[rows, cols] = split(v)

        @pl.loop(0, 2)
        def _(h):
            cols = pl.ds(pl.multiple_of(h * 256, 256), 256)
            v = dot3(ah[...], al[...], wh[:, cols], wl[:, cols])
            for k in range(NX):
                mine[zo * NX + k, :, cols] = v[PIECE * k : PIECE * (k + 1), :]

    tile_row = lax.broadcasted_iota(jnp.int32, (PANEL, PANEL), 0)
    tile_col = lax.broadcasted_iota(jnp.int32, (PANEL, PANEL), 1)
    low, diagonal = tile_row >= tile_col, tile_row == tile_col
    spare = lax.broadcasted_iota(jnp.int32, (8, PANEL), 0)

    def pair_block(i, j):
        return vc[PANEL * i : PANEL * (i + 1), :] + ve_row_ref[0:1, PANEL * j : PANEL * (j + 1)] - self_energy

    def products(kind, a, b, dst, add):
        rh[...], rl[...] = split(a[...])
        th[...], tl[...] = split(b[...].T)
        if kind == OWN:

            def put(at, v):
                rows = slice(at, at + v.shape[0])
                dst[rows, :] = dst[rows, :] + v if add else v

            extra = jnp.zeros((8, PANEL), F32)
            first = None
            for j in range(PANELS):
                at, cols = PANEL * j, slice(PANEL * j, PANEL * (j + 1))
                v = dot3(th[at:, :], tl[at:, :], rh[:, cols], rl[:, cols])
                if j + 1 < PANELS:
                    put(PANEL * OFF.index((j, j + 1)), v[PANEL:, :])
                if j % 2 == 0:
                    first = v[:PANEL, :]
                else:
                    second = v[:PANEL, :]
                    put(PANEL * (len(OFF) + j // 2), jnp.where(low, first, second))
                    d = jnp.sum(jnp.where(diagonal, second, 0.0), axis=0, keepdims=True)
                    extra = jnp.where(spare == j // 2, d, extra)
            put(SPARE, extra)
        else:

            @pl.loop(0, 2)
            def _(h):
                rows = pl.ds(pl.multiple_of(h * 256, 256), 256)
                v = dot3(th[rows, :], tl[rows, :], rh[...], rl[...])
                dst[rows, :] = dst[rows, :] + v if add else v

    def partial_products(kind, n):
        x_arrived(kind, n)
        if kind == OWN:
            products(OWN, own.at[n - 2], own.at[n - 2], ps.at[n - 2], False)
        else:
            products(PAR, own.at[n - 2], par.at[n - 2], pc.at[n - 2], False)

    def accumulate(kind, p, r, h):
        dst, src = ((ps, rs), (pc, rc))[kind]
        rows = part(kind, h)
        dst[p, rows, :] = dst[p, rows, :] + src[r, rows, :]

    def to_amplitude(kind, h):
        if kind == OWN:

            def divide(at, pair):
                rows = slice(at, at + pair.shape[0])
                ps[5, rows, :] = (ps[5, rows, :] + rs[3, rows, :] + rs[4, rows, :]) / pair

            for b, (j, i) in enumerate(OFF):
                if CUTS[OWN][h] <= PANEL * b < CUTS[OWN][h + 1]:
                    divide(PANEL * b, pair_block(i, j))
            if h == PARTS - 1:
                extra = jnp.ones((8, PANEL), F32)
                for k in range(PANELS // 2):
                    i, j = 2 * k, 2 * k + 1
                    divide(PANEL * (len(OFF) + k), jnp.where(low, pair_block(i, i), pair_block(j, j)))
                    ve = ve_row_ref[0:1, PANEL * j : PANEL * (j + 1)]
                    extra = jnp.where(spare == k, ve + ve - self_energy, extra)
                divide(SPARE, extra)
        else:
            rows = part(PAR, h)
            for j in range(PANELS):
                cols = slice(PANEL * j, PANEL * (j + 1))
                pair = vc[rows, :] + ve_row_ref[0:1, cols] - cross_energy
                pc[5, rows, cols] = (pc[5, rows, cols] + rc[3, rows, cols] + rc[4, rows, cols]) / pair

    def unpack(kind, p):
        own_t, other_t = ((ps, rs), (pc, rc))[kind]
        t = own_t.at[5] if p == 5 else other_t.at[(5, 6, 0, 1, 2)[p]]
        if kind == OWN:

            def put(i, j, v):
                at = slice(PANEL * i, PANEL * (i + 1)), slice(PANEL * j, PANEL * (j + 1))
                fh[at], fl[at] = split(v)

            for b, (j, i) in enumerate(OFF):
                v = t[PANEL * b : PANEL * (b + 1), :]
                put(i, j, v)
                put(j, i, v.T)
            for k in range(PANELS // 2):
                at = PANEL * (len(OFF) + k)
                v = t[at : at + PANEL, :]
                w = v.T
                put(2 * k, 2 * k, jnp.where(low, v, w))
                d = t[SPARE + k : SPARE + k + 1, :]
                put(2 * k + 1, 2 * k + 1, jnp.where(diagonal, d, jnp.where(low, w, v)))
        else:
            fh[...], fl[...] = split(t[...])

    def apply(kind, src, dst):
        rh[...], rl[...] = split(src[...])

        @pl.loop(0, 2)
        def _(h):
            cols = pl.ds(pl.multiple_of(h * 256, 256), 256)
            v = dot3(rh[...], rl[...], fh[:, cols], fl[:, cols])
            for k in range(NX):
                w = v[PIECE * k : PIECE * (k + 1), :]
                dst[k, :, cols] = w if kind == OWN else dst[k, :, cols] + w

    def density(kind, p):
        unpack(kind, p)
        apply(kind, (own, par)[kind].at[p], dense(p + 2))

    def density_leaf(kind, p):
        unpack(kind, p)
        apply(kind, raw.at[kind, p], leaf(p))
        if kind == PAR:
            start(end_copies(OUT, p))
        apply(kind, (own, par)[kind].at[p], dense(p + 2))

    def begin_occ():
        for d in range(1, GROUPS):

            @pl.loop(0, CAPACITY)
            def _(s):
                pool[(d - 1) * CAPACITY + s] = mine[table_s[d, s]]

            for h in range(2):
                occ_copy(d, h).start()

        @pl.loop(0, CAPACITY)
        def _(s):
            inbound[s] = mine[table_s[0, s]]

    def inward(kind, between):
        p = (ps, pc)[kind]
        for j in range(2):
            partial_products(kind, 2 + j)
            end_arrived(kind, j)
            products(kind, raw.at[OWN, j], raw.at[kind, j], p.at[j], True)
            for h in range(PARTS):
                send(kind, 2 + j, h)
            between(j)
        for n in (4, 5):
            partial_products(kind, n)
        between(2)
        for h in range(PARTS):
            for j in range(2):
                arrived(kind, 2 + j, h)
                accumulate(kind, 2 + j, j, h)
                send(kind, 4 + j, h)
        for n in (6, 7):
            partial_products(kind, n)
        between(3)
        for h in range(PARTS):
            arrived(kind, 4, h)
            accumulate(kind, 4, 2, h)
            send(kind, 6, h)
        between(4)
        for h in range(PARTS):
            arrived(kind, 5, h)
            arrived(kind, 6, h)
            to_amplitude(kind, h)
            send(kind, 7, h)
            send(kind, 8, h)

    first_product(0)
    first_product(2)
    pl.semaphore_wait(barrier, len(near) + GROUPS - 1)
    start(end_copies(OWN, 0))
    start(x_copies(OWN, 2))
    first_product(1)
    start(end_copies(OWN, 1))
    first_product(3)
    start(x_copies(OWN, 3))

    @pl.loop(4, NZ)
    def _(n):
        first_product(n)

    to_table.wait()
    to_place.wait()
    begin_occ()

    def rest(k):
        if k < 2:
            start(x_copies(OWN, 4 + k))
            start(x_copies(OWN, 6 + k))

    inward(OWN, rest)

    for n in range(2):
        end_sent(OWN, n)

    @pl.loop(2, NZ)
    def _(n):
        x_sent(OWN, n)

    def take_partners(n):
        zo = owner_z(n)
        for k in range(NX):
            mine[zo * NX + k] = inbound[place_s[0, occ * GO + zo * NX + k]]

    pass_on(OWN, (7, 9), (8, 10))
    for d in range(1, GROUPS):
        for h in range(2):
            occ_copy(d, h).wait_recv()
            occ_copy(d, h).wait_send()
    take_partners(0)
    start(end_copies(PAR, 0))
    take_partners(2)
    start(x_copies(PAR, 2))
    take_partners(1)
    start(end_copies(PAR, 1))
    take_partners(3)
    start(x_copies(PAR, 3))
    pass_on(OWN, (9, 11))

    @pl.loop(4, NZ)
    def _(n):
        take_partners(n)
        start(x_copies(PAR, n))

    def between(k):
        if k == 0:
            density(OWN, 5)
        if k == 2:
            density(OWN, 4)
            density(OWN, 3)
        if k == 3:
            for h in range(PARTS):
                arrived(OWN, 10, h)
            density_leaf(OWN, 1)
            density(OWN, 2)
        if k == 4:
            for h in range(PARTS):
                arrived(OWN, 11, h)
            density_leaf(OWN, 0)

    inward(PAR, between)

    pass_on(PAR, (7, 9), (8, 10))
    density(PAR, 5)
    start(x_copies(OUT, 7))
    pass_on(PAR, (9, 11))
    density(PAR, 4)
    start(x_copies(OUT, 6))
    density(PAR, 3)
    start(x_copies(OUT, 5))
    for h in range(PARTS):
        arrived(PAR, 10, h)
    density_leaf(PAR, 1)
    start(x_copies(OUT, 3))
    density(PAR, 2)
    start(x_copies(OUT, 4))
    for h in range(PARTS):
        arrived(PAR, 11, h)
    density_leaf(PAR, 0)
    start(x_copies(OUT, 2))

    for kind in (OWN, PAR):
        for t in range(2, 12):
            for h in range(PARTS):
                z_copy(kind, t, h).wait_send()

    for n in range(2):
        end_sent(PAR, n)
        end_arrived(OUT, n)
        end_sent(OUT, n)

    @pl.loop(2, NZ)
    def _(n):
        x_sent(PAR, n)
        x_arrived(OUT, n)
        x_sent(OUT, n)


def local(half_integrals, virtual_orbitals, occupied_energy, virtual_energy, partners):
    slices, size, atoms = half_integrals.shape
    width = virtual_orbitals.shape[1]
    total = partners.shape[0]
    vmem = lambda *s: pltpu.VMEM(s, F32)
    half_vmem = lambda *s: pltpu.VMEM(s, BF16)
    dma = pltpu.SemaphoreType.DMA
    smem = pl.BlockSpec(memory_space=pltpu.SMEM)
    whole = pl.BlockSpec(memory_space=pltpu.VMEM)
    hbm = pl.BlockSpec(memory_space=pl.ANY)
    flat = partners.reshape(total)
    out = pl.pallas_call(
        kernel,
        out_shape=jax.ShapeDtypeStruct((size, slices, width), F32),
        in_specs=[smem, smem, whole, whole, hbm, whole, whole],
        out_specs=hbm,
        scratch_shapes=[
            vmem(size, slices, width),
            vmem((GROUPS - 1) * CAPACITY, slices, width),
            vmem(GROUPS * CAPACITY, slices, width),
            vmem(NZ - 2, ROWS, WIDTH),
            vmem(NZ - 2, ROWS, WIDTH),
            vmem(2, 2, ROWS, WIDTH),
            vmem(6, PACKED, PANEL),
            vmem(7, PACKED, PANEL),
            vmem(6, WIDTH, WIDTH),
            vmem(7, WIDTH, WIDTH),
            half_vmem(WIDTH, ROWS),
            half_vmem(WIDTH, ROWS),
            half_vmem(ROWS, WIDTH),
            half_vmem(ROWS, WIDTH),
            half_vmem(WIDTH, WIDTH),
            half_vmem(WIDTH, WIDTH),
            vmem(size // SUB, atoms // PANEL, slices, SUB, PANEL),
            half_vmem(atoms, width),
            half_vmem(atoms, width),
            half_vmem(ROWS, atoms),
            half_vmem(ROWS, atoms),
            vmem(WIDTH, PANEL),
            pltpu.VMEM((GROUPS, PANEL), jnp.int32),
            pltpu.VMEM((8, total), jnp.int32),
            pltpu.SMEM((GROUPS, PANEL), jnp.int32),
            pltpu.SMEM((8, total), jnp.int32),
            dma((3, NZ, NX)),
            dma((3, NZ, NX)),
            dma((GROUPS, 2)),
            dma((GROUPS, 2)),
            dma((2, 12, PARTS)),
            dma((2, 12, PARTS)),
            dma((size // SUB + 1, atoms // PANEL)),
        ],
        compiler_params=pltpu.CompilerParams(
            collective_id=0, has_side_effects=True, vmem_limit_bytes=62 * 1024 * 1024
        ),
    )(
        flat,
        occupied_energy,
        flat[None, :],
        partners,
        half_integrals,
        virtual_orbitals,
        virtual_energy[None, :],
    )
    return jnp.transpose(out, (1, 0, 2))


def solution(mesh):
    return jax.shard_map(
        local,
        mesh=mesh,
        in_specs=(P("aux", "occ", None), P(), P(), P(), P()),
        out_specs=P("aux", "occ", None),
        check_vma=False,
    )
```
